256 devices in a mesh: sens: 16 (over z, y_lo), unk: 16 (over x, y_hi, core).
Axes of the slice: x: 4, y: 4 (y_hi: 2, y_lo: 2; y = y_hi * 2 + y_lo), z: 8, core: 2. Of those that a mesh axis runs over, the one named last changes fastest.
Arguments:
- signals: float32 [512, 4, 256], P('sens', None, 'unk'), may hold values from -6 to 6
- kernel: float32 [512, 32, 16384], P('sens', None, 'unk'), may hold values from -0.0234375 to 0.0234375
- tap_weights: float32 [17, 16384], P(None, 'unk'), may hold values from -1.5 to 1.5
Outputs:
- hessian_action: float32 [512, 4, 256], P('sens', None, 'unk')
The draws below stay inside these ranges and needn't reach their ends.
All inputs are finite; a program needn't handle non-finite values.
Results may differ from the reference program's by a relative error of at most 0.00008.
Values sent between devices are 32-bit elements; how exact they have to be, the bound alone decides.
No kernel may reach another device: no remote copies, remote signals or barrier semaphores. Data moves between devices by JAX's collectives and lax.ppermute only.
A program may use at most 64 MiB of HBM per device.

```python
import jax
import jax.numpy as jnp
from jax import lax

LAGS = 32
T_SIZE = 256
NVEC = 4
HALF = 8
TAPS = 17
SENSORS = 512
UNKNOWNS = 16384


def shard_levels(own_key, shape, cuts, least, largest):
    gain = 1.0
    for position, blocks in cuts:
        heights = jax.random.uniform(jax.random.fold_in(jax.random.fold_in(own_key, 6), position), (blocks,), jnp.float32, least / len(cuts), largest / len(cuts))
        gain = gain * jnp.repeat(jnp.exp(heights), shape[position] // blocks).reshape((-1,) + (1,) * (len(shape) - 1 - position))
    return gain


def gaussian(own_key, shape, deviation, limit, split=(), dtype=jnp.bfloat16):
    array = deviation * jax.random.normal(own_key, shape, jnp.float32)
    if split:
        array = array * shard_levels(own_key, shape, split, -0.22, 0.18)
    return jnp.clip(array, -limit, limit).astype(dtype)


def setup_inputs(seed: int = 0) -> dict:
    streams_of = jax.random.split(jax.random.key(seed), 4)
    signals = gaussian(streams_of[0], (SENSORS, NVEC, T_SIZE), 1.0, 6.0, ((0, 16), (2, 16)), jnp.float32)
    kernel = gaussian(streams_of[1], (SENSORS, LAGS, UNKNOWNS), (LAGS * (SENSORS + UNKNOWNS) // 8) ** -0.5, 0.0234375, ((0, 16), (2, 16)), jnp.float32)
    tap_weights = gaussian(streams_of[2], (TAPS, UNKNOWNS), TAPS ** -0.5, 1.5, ((1, 16),), jnp.float32)
    return dict(signals=signals, kernel=kernel, tap_weights=tap_weights)


def hankel(signals, lag_count):
    steps_count = signals.shape[2]
    padded = jnp.pad(signals, ((0, 0), (0, 0), (0, lag_count)))
    return jnp.stack([padded[:, :, offset:offset + steps_count] for offset in range(lag_count)], axis=1)


def skew_sum(product):
    sens_rows, vectors, lag_count, steps_count = product.shape
    padded = jnp.pad(product, ((0, 0), (0, 0), (0, 0), (0, lag_count)))
    flattened = padded.reshape(sens_rows, vectors, lag_count * (steps_count + lag_count))
    flattened = flattened[:, :, :lag_count * (steps_count + lag_count - 1)]
    sheared = flattened.reshape(sens_rows, vectors, lag_count, steps_count + lag_count - 1)
    return jnp.sum(sheared[..., :steps_count], axis=2)


def smooth_time(series, tap_weights, half_width):
    steps_count = series.shape[2]
    padded = jnp.pad(series, ((0, 0), (0, 0), (half_width, half_width)))
    result = jnp.zeros(series.shape, jnp.float32)
    for tap_index in range(2 * half_width + 1):
        result = result + tap_weights[tap_index][:, None, None] * padded[:, :, tap_index:tap_index + steps_count]
    return result


def reference(signals, kernel, tap_weights):
    window = hankel(signals, LAGS)
    adjoint = jnp.einsum('slu,slbt->ubt', kernel, window, precision=lax.Precision.HIGHEST)
    smoothed = smooth_time(adjoint, tap_weights, HALF)
    product = jnp.einsum('slu,ubt->sblt', kernel, smoothed, precision=lax.Precision.HIGHEST)
    return skew_sum(product)
```

```python
import functools

import jax
import jax.numpy as jnp
from jax import lax
from jax.experimental import pallas as pl
from jax.experimental.pallas import tpu as pltpu
from jax.sharding import Mesh, PartitionSpec as P


CHUNKS = 2
UNK = ("x", "yh", "c")
HIGH = lax.Precision.HIGH


def ring(size, step):
    return [(i, (i + step) % size) for i in range(size)]


def swap(value, axis):
    return lax.ppermute(value, axis, [(0, 1), (1, 0)])


def mirror(steps):
    row = lax.broadcasted_iota(jnp.int32, (steps, steps), 0)
    column = lax.broadcasted_iota(jnp.int32, (steps, steps), 1)
    return jnp.where(row + column == steps - 1, 1.0, 0.0)


def window_kernel(series_ref, window_ref, rows_ref, *, sensors, vectors, lags, steps):
    rows_ref[...] = lax.dot_general(
        series_ref[...], mirror(steps), (((0,), (0,)), ((), ())), precision=lax.Precision.HIGHEST
    )
    lane = lax.broadcasted_iota(jnp.int32, (lags, steps), 1)
    lag = lax.broadcasted_iota(jnp.int32, (lags, steps), 0)
    keep = lane >= lag

    def body(s, carry):
        for b in range(vectors):
            row = jnp.broadcast_to(rows_ref[pl.ds(s * vectors + b, 1), :], (lags, steps))
            rolled = pltpu.roll(row, 0, 1, stride=1, stride_axis=0)
            window_ref[pl.ds(s * lags, lags), b * steps : (b + 1) * steps] = jnp.where(
                keep, rolled, 0.0
            )
        return carry

    lax.fori_loop(0, sensors, body, 0)


def window_of(series, lags, vectors):
    steps, columns = series.shape
    sensors = columns // vectors
    return pl.pallas_call(
        functools.partial(
            window_kernel, sensors=sensors, vectors=vectors, lags=lags, steps=steps
        ),
        out_shape=jax.ShapeDtypeStruct((sensors * lags, vectors * steps), jnp.float32),
        in_specs=[pl.BlockSpec(memory_space=pltpu.VMEM)],
        out_specs=pl.BlockSpec(memory_space=pltpu.VMEM),
        scratch_shapes=[pltpu.VMEM((columns, steps), jnp.float32)],
        name="window",
    )(series)


def skew_kernel(product_ref, out_ref, rows_ref, *, sensors, vectors, lags, steps):
    lane = lax.broadcasted_iota(jnp.int32, (lags, steps), 1)
    lag = lax.broadcasted_iota(jnp.int32, (lags, steps), 0)
    keep = lane >= lag

    def body(s, carry):
        for b in range(vectors):
            tile = product_ref[pl.ds(s * lags, lags), b * steps : (b + 1) * steps]
            rolled = pltpu.roll(tile, 0, 1, stride=1, stride_axis=0)
            rows_ref[pl.ds(s * vectors + b, 1), :] = jnp.sum(
                jnp.where(keep, rolled, 0.0), axis=0, keepdims=True
            )
        return carry

    lax.fori_loop(0, sensors, body, 0)
    out_ref[...] = rows_ref[...].T


def skew_of(product, lags, vectors):
    rows, columns = product.shape
    steps = columns // vectors
    sensors = rows // lags
    return pl.pallas_call(
        functools.partial(
            skew_kernel, sensors=sensors, vectors=vectors, lags=lags, steps=steps
        ),
        out_shape=jax.ShapeDtypeStruct((steps, sensors * vectors), jnp.float32),
        in_specs=[pl.BlockSpec(memory_space=pltpu.VMEM)],
        out_specs=pl.BlockSpec(memory_space=pltpu.VMEM),
        scratch_shapes=[pltpu.VMEM((sensors * vectors, steps), jnp.float32)],
        name="skew",
    )(product)


def smooth_kernel(series_ref, taps_ref, out_ref, *, vectors, steps):
    taps, rows = taps_ref.shape
    half = (taps - 1) // 2
    weights = taps_ref[...].T
    turn = mirror(steps)
    lane = lax.broadcasted_iota(jnp.int32, (rows, steps), 1)
    for b in range(vectors):
        block = jnp.dot(
            series_ref[:, b * steps : (b + 1) * steps], turn, precision=lax.Precision.HIGHEST
        )
        total = weights[:, half : half + 1] * block
        for k in range(taps):
            move = k - half
            if move == 0:
                continue
            moved = pltpu.roll(block, (-move) % steps, 1)
            inside = lane < steps - move if move > 0 else lane >= -move
            total = total + weights[:, k : k + 1] * jnp.where(inside, moved, 0.0)
        out_ref[:, b * steps : (b + 1) * steps] = total


def smooth_of(series, taps, vectors):
    rows, columns = series.shape
    return pl.pallas_call(
        functools.partial(smooth_kernel, vectors=vectors, steps=columns // vectors),
        out_shape=jax.ShapeDtypeStruct(series.shape, jnp.float32),
        in_specs=[pl.BlockSpec(memory_space=pltpu.VMEM)] * 2,
        out_specs=pl.BlockSpec(memory_space=pltpu.VMEM),
        name="smooth",
    )(series, taps)


def reduce_over_z(partial):
    size = partial.shape[0]
    far = size // 2
    z = lax.axis_index("z")
    cut = partial.shape[1] // 2

    def slot(offset):
        return lax.dynamic_index_in_dim(partial, lax.rem(z + offset + size, size), 0, False)

    across = slot(far)
    up = lax.ppermute(across[:cut], "z", ring(size, 1))
    down = lax.ppermute(across[cut:], "z", ring(size, -1))
    own = slot(far - 1)
    up = jnp.concatenate([own[:cut] + up, own[cut:]])
    own = slot(1 - far)
    down = jnp.concatenate([own[:cut], own[cut:] + down])
    for offset in range(far - 2, -1, -1):
        up = lax.ppermute(up, "z", ring(size, 1))
        down = lax.ppermute(down, "z", ring(size, -1))
        if offset:
            up = up + slot(offset)
            down = down + slot(-offset)
    return (slot(0) + up) + down


def gather_over_z(own):
    size = lax.axis_size("z")
    far = size // 2
    z = lax.axis_index("z")
    rows = own.shape[0]
    cut = rows // 2
    up, down = own, own
    parts = {0: own}
    for step in range(1, far):
        up = lax.ppermute(up, "z", ring(size, 1))
        down = lax.ppermute(down, "z", ring(size, -1))
        parts[-step], parts[step] = up, down
    up = lax.ppermute(up[:cut], "z", ring(size, 1))
    down = lax.ppermute(down[cut:], "z", ring(size, -1))
    whole = jnp.zeros((size, *own.shape), own.dtype)
    parts[far] = jnp.concatenate([up, down])
    for offset, part in parts.items():
        whole = lax.dynamic_update_index_in_dim(
            whole, part, lax.rem(z + offset + size, size), 0
        )
    return whole.reshape(size * rows, own.shape[1])


def gather_series(series):
    both = jnp.concatenate([series, swap(series, "yl")], axis=1)
    c = lax.axis_index("c")
    other = swap(both, "c")
    both = jnp.concatenate([jnp.where(c == 0, both, other), jnp.where(c == 0, other, both)])
    y = lax.axis_index("yh")
    other = swap(both, "yh")
    both = jnp.concatenate([jnp.where(y == 0, both, other), jnp.where(y == 0, other, both)])
    x = lax.axis_index("x")
    size = lax.axis_size("x")
    whole = jnp.zeros((size, *both.shape), both.dtype)
    for step in range(size):
        part = both if step == 0 else lax.ppermute(both, "x", ring(size, step))
        whole = lax.dynamic_update_index_in_dim(whole, part, lax.rem(x - step + size, size), 0)
    return whole.reshape(size * both.shape[0], both.shape[1])


def reduce_result(result):
    columns = result.shape[1] // 2
    result = result[:, :columns] + swap(result[:, columns:], "yl")
    size = lax.axis_size(UNK)
    pieces = result.reshape(size, result.shape[0] // size, columns)
    return jnp.sum(lax.all_to_all(pieces, UNK, 0, 0, tiled=True), axis=0)


def on_device(signals, kernel, tap_weights):
    sensors, vectors, steps_here = signals.shape
    lags, unknowns = kernel.shape[1:]
    yl, z = lax.axis_index("yl"), lax.axis_index("z")
    z_size = lax.axis_size("z")
    width = unknowns // (2 * CHUNKS)

    def columns_of(array, chunk, half):
        return lax.dynamic_slice_in_dim(array, chunk * 2 * width + half * width, width, 1)

    matrix = kernel.reshape(sensors * lags, unknowns)
    given = [swap(columns_of(matrix, chunk, 1 - yl), "yl") for chunk in range(CHUNKS)]
    blocks = [
        jnp.concatenate([columns_of(matrix, chunk, yl), given[chunk]])
        for chunk in range(CHUNKS)
    ]
    series = gather_series(signals.reshape(sensors * vectors, steps_here).T)
    window = window_of(series, lags, vectors)
    slot = width // z_size
    smoothed = []
    for chunk in range(CHUNKS):
        partial = lax.dot_general(
            blocks[chunk], window, (((0,), (0,)), ((), ())), precision=HIGH
        )
        own = reduce_over_z(partial.reshape(z_size, slot, partial.shape[1]))
        taps = lax.dynamic_slice_in_dim(
            columns_of(tap_weights, chunk, yl), z * slot, slot, 1
        )
        smoothed.append(gather_over_z(smooth_of(own, taps, vectors)))
    product = sum(
        jnp.dot(block, part, precision=HIGH) for block, part in zip(blocks, smoothed)
    )
    result = reduce_result(skew_of(product, lags, vectors))
    return result.T.reshape(sensors, vectors, steps_here)


def solution(mesh):
    sens, unk = mesh.devices.shape
    fine = Mesh(mesh.devices.reshape(sens // 2, 2, unk // 4, 2, 2), ("z", "yl", *UNK))
    sensor_axes = ("z", "yl")
    return jax.shard_map(
        on_device,
        mesh=fine,
        in_specs=(P(sensor_axes, None, UNK), P(sensor_axes, None, UNK), P(None, UNK)),
        out_specs=P(sensor_axes, None, UNK),
        check_vma=False,
    )
```

```python
import functools

import jax
import jax.numpy as jnp
from jax import lax
from jax.experimental import pallas as pl
from jax.experimental.pallas import tpu as pltpu
from jax.sharding import Mesh, PartitionSpec as P


UNK = ("x", "yh", "c")
PAIRS = ((4, 0), (3, 5), (2, 6), (1, 7))


def ring(size, step):
    return [(i, (i + step) % size) for i in range(size)]


def swap(value, axis):
    return lax.ppermute(value, axis, [(0, 1), (1, 0)])


def split(value):
    high = value.astype(jnp.bfloat16)
    return high, (value - high.astype(jnp.float32)).astype(jnp.bfloat16)


def mirror(steps):
    row = lax.broadcasted_iota(jnp.int32, (steps, steps), 0)
    column = lax.broadcasted_iota(jnp.int32, (steps, steps), 1)
    return jnp.where(row + column == steps - 1, 1.0, 0.0)


def window_kernel(series_ref, high_ref, low_ref, rows_ref, *, group, vectors, lags, steps):
    block = pl.program_id(0)

    @pl.when(block == 0)
    def _():
        rows_ref[...] = lax.dot_general(
            series_ref[...], mirror(steps), (((0,), (0,)), ((), ())),
            precision=lax.Precision.HIGHEST,
        )

    lane = lax.broadcasted_iota(jnp.int32, (lags, steps), 1)
    lag = lax.broadcasted_iota(jnp.int32, (lags, steps), 0)
    keep = lane >= lag
    for s in range(group):
        for b in range(vectors):
            row = rows_ref[pl.ds((block * group + s) * vectors + b, 1), :]
            rolled = pltpu.roll(jnp.broadcast_to(row, (lags, steps)), 0, 1, stride=1, stride_axis=0)
            place = (slice(s * lags, (s + 1) * lags), slice(b * steps, (b + 1) * steps))
            high_ref[place], low_ref[place] = split(jnp.where(keep, rolled, 0.0))


def window_of(series, lags, vectors):
    steps, columns = series.shape
    sensors = columns // vectors
    group = 4
    return pl.pallas_call(
        functools.partial(
            window_kernel, group=group, vectors=vectors, lags=lags, steps=steps
        ),
        grid=(sensors // group,),
        out_shape=[jax.ShapeDtypeStruct((sensors * lags, vectors * steps), jnp.bfloat16)] * 2,
        in_specs=[pl.BlockSpec((steps, columns), lambda i: (0, 0))],
        out_specs=[pl.BlockSpec((group * lags, vectors * steps), lambda i: (i, 0))] * 2,
        scratch_shapes=[pltpu.VMEM((columns, steps), jnp.float32)],
        name="window",
    )(series)


def pair_kernel(scalars_ref, kernel_ref, *out_refs):
    z = scalars_ref[1]
    slots = 2 * len(out_refs)
    lanes = out_refs[0].shape[1]
    slot = lanes // 2
    lane = lax.broadcasted_iota(jnp.int32, out_refs[0].shape, 1)

    def half_of(offset, high):
        place = lax.rem(z + offset, slots)
        start = pl.multiple_of(place // 2 * lanes, lanes)
        shift = lax.rem(lax.rem(place, 2) + high, 2) * slot
        return pltpu.roll(kernel_ref[:, pl.ds(start, lanes)], shift, 1)

    for out_ref, (low, high) in zip(out_refs, PAIRS):
        out_ref[...] = jnp.where(lane < slot, half_of(low, 0), half_of(high, 1))


def pairs_of(matrix, half, z):
    rows, unknowns = matrix.shape
    width = unknowns // 2
    count = len(PAIRS)
    block = rows // 4
    return pl.pallas_call(
        pair_kernel,
        grid_spec=pltpu.PrefetchScalarGridSpec(
            num_scalar_prefetch=1,
            grid=(rows // block,),
            in_specs=[pl.BlockSpec((block, width), lambda i, scalars: (i, scalars[0]))],
            out_specs=[pl.BlockSpec((block, width // count), lambda i, scalars: (i, 0))] * count,
        ),
        out_shape=[jax.ShapeDtypeStruct((rows, width // count), jnp.float32)] * count,
        name="pairs",
    )(jnp.stack([half, z]).astype(jnp.int32), matrix)


def three_pass(high, low, right_high, right_low):
    dot = functools.partial(jnp.dot, preferred_element_type=jnp.float32)
    rows = high.shape[0]
    both = dot(jnp.concatenate([high, low]), right_high)
    return both[:rows] + both[rows:] + dot(high, right_low)


def adjoint_kernel(
    kept_ref, given_ref, kept_high_ref, kept_low_ref, given_high_ref, given_low_ref, out_ref
):
    kept_high, kept_low = split(kept_ref[...].T)
    given_high, given_low = split(given_ref[...].T)
    total = three_pass(kept_high, kept_low, kept_high_ref[...], kept_low_ref[...])
    total = total + three_pass(given_high, given_low, given_high_ref[...], given_low_ref[...])
    first = pl.program_id(0) == 0

    @pl.when(first)
    def _():
        out_ref[...] = total

    @pl.when(jnp.logical_not(first))
    def _():
        out_ref[...] += total


def adjoint_of(kept, given, window):
    rows, unknowns = kept.shape
    columns = window[0].shape[1]
    count = 4
    block = rows // count
    first = pl.BlockSpec((block, columns), lambda i: (i, 0))
    second = pl.BlockSpec((block, columns), lambda i: (i + count, 0))
    thin = pl.BlockSpec((block, unknowns), lambda i: (i, 0))
    return pl.pallas_call(
        adjoint_kernel,
        grid=(count,),
        out_shape=jax.ShapeDtypeStruct((unknowns, columns), jnp.float32),
        in_specs=[thin, thin, first, first, second, second],
        out_specs=pl.BlockSpec((unknowns, columns), lambda i: (0, 0)),
        name="adjoint",
    )(kept, given, *window, *window)


def fill(high_ref, low_ref, parts):
    start = 0
    for part in parts:
        here = slice(start, start + part.shape[0])
        high_ref[here, :], low_ref[here, :] = split(part[...])
        start += part.shape[0]


def multiply(kernel_refs, high_ref, low_ref):
    high, low = split(jnp.concatenate([ref[...] for ref in kernel_refs], axis=1))
    return three_pass(high, low, high_ref[...], low_ref[...])


def early_kernel(k0, k1, p0, p1, p2, p3, out_ref, high_ref, low_ref):
    @pl.when(pl.program_id(0) == 0)
    def _():
        fill(high_ref, low_ref, (p0, p1, p2, p3))

    out_ref[...] = multiply((k0, k1), high_ref, low_ref)


def early_of(kernels, parts):
    rows, width = kernels[0].shape
    columns = parts[0].shape[1]
    block = 256
    return pl.pallas_call(
        early_kernel,
        grid=(rows // block,),
        out_shape=jax.ShapeDtypeStruct((rows, columns), jnp.float32),
        in_specs=[pl.BlockSpec((block, width), lambda i: (i, 0))] * 2
        + [pl.BlockSpec(part.shape, lambda i: (0, 0)) for part in parts],
        out_specs=pl.BlockSpec((block, columns), lambda i: (i, 0)),
        scratch_shapes=[pltpu.VMEM((2 * width, columns), jnp.bfloat16)] * 2,
        name="early",
    )(*kernels, *parts)


def forward_kernel(
    k0, k1, p0, p1, p2, p3, before_ref, out_ref, high_ref, low_ref, product_ref, rows_ref,
    *, group, vectors, lags, steps,
):
    step = pl.program_id(0)

    @pl.when(step == 0)
    def _():
        fill(high_ref, low_ref, (p0, p1, p2, p3))
        product_ref[1] = jnp.zeros(product_ref.shape[1:], jnp.float32)

    lane = lax.broadcasted_iota(jnp.int32, (lags, steps), 1)
    lag = lax.broadcasted_iota(jnp.int32, (lags, steps), 0)
    keep = lane >= lag
    block = jnp.maximum(step - 1, 0)
    ready = lax.rem(step + 1, 2)
    for s in range(group):
        for b in range(vectors):
            tile = product_ref[ready, s * lags : (s + 1) * lags, b * steps : (b + 1) * steps]
            rolled = pltpu.roll(tile, 0, 1, stride=1, stride_axis=0)
            rows_ref[pl.ds((block * group + s) * vectors + b, 1), :] = jnp.sum(
                jnp.where(keep, rolled, 0.0), axis=0, keepdims=True
            )
    product_ref[lax.rem(step, 2)] = before_ref[...] + multiply((k0, k1), high_ref, low_ref)

    @pl.when(step == pl.num_programs(0) - 1)
    def _():
        out_ref[...] = rows_ref[...].T


def forward_of(kernels, parts, before, lags, vectors):
    rows, width = kernels[0].shape
    columns = before.shape[1]
    steps = columns // vectors
    sensors = rows // lags
    group = 8
    last = sensors // group - 1

    def block_of(i):
        return (jnp.minimum(i, last), 0)

    return pl.pallas_call(
        functools.partial(forward_kernel, group=group, vectors=vectors, lags=lags, steps=steps),
        grid=(last + 2,),
        out_shape=jax.ShapeDtypeStruct((steps, sensors * vectors), jnp.float32),
        in_specs=[pl.BlockSpec((group * lags, width), block_of)] * 2
        + [pl.BlockSpec(part.shape, lambda i: (0, 0)) for part in parts]
        + [pl.BlockSpec((group * lags, columns), block_of)],
        out_specs=pl.BlockSpec((steps, sensors * vectors), lambda i: (0, 0)),
        scratch_shapes=[
            pltpu.VMEM((2 * width, columns), jnp.bfloat16),
            pltpu.VMEM((2 * width, columns), jnp.bfloat16),
            pltpu.VMEM((2, group * lags, columns), jnp.float32),
            pltpu.VMEM((sensors * vectors, steps), jnp.float32),
        ],
        name="forward",
    )(*kernels, *parts, before)


def smooth_kernel(own_ref, up_ref, down_ref, taps_ref, out_ref, *, vectors, steps):
    taps, rows = taps_ref.shape
    half = (taps - 1) // 2
    weights = taps_ref[...].T
    turn = mirror(steps)
    lane = lax.broadcasted_iota(jnp.int32, (rows, steps), 1)
    for b in range(vectors):
        here = (slice(None), slice(b * steps, (b + 1) * steps))
        block = jnp.dot(
            own_ref[here] + up_ref[here] + down_ref[here], turn, precision=lax.Precision.HIGHEST
        )
        total = weights[:, half : half + 1] * block
        for k in range(taps):
            move = k - half
            if move == 0:
                continue
            moved = pltpu.roll(block, (-move) % steps, 1)
            inside = lane < steps - move if move > 0 else lane >= -move
            total = total + weights[:, k : k + 1] * jnp.where(inside, moved, 0.0)
        out_ref[:, b * steps : (b + 1) * steps] = total


def smooth_of(addends, taps, vectors):
    columns = addends[0].shape[1]
    return pl.pallas_call(
        functools.partial(smooth_kernel, vectors=vectors, steps=columns // vectors),
        out_shape=jax.ShapeDtypeStruct(addends[0].shape, jnp.float32),
        in_specs=[pl.BlockSpec(memory_space=pltpu.VMEM)] * 4,
        out_specs=pl.BlockSpec(memory_space=pltpu.VMEM),
        name="smooth",
    )(*addends, taps)


def reduce_over_z(partial):
    size = lax.axis_size("z")
    far = size // 2
    cut = partial[far].shape[0] // 2
    up = lax.ppermute(partial[far][:cut], "z", ring(size, 1))
    down = lax.ppermute(partial[far][cut:], "z", ring(size, -1))
    above, below = partial[far - 1], partial[1 - far]
    up = jnp.concatenate([above[:cut] + up, above[cut:]])
    down = jnp.concatenate([below[:cut], below[cut:] + down])
    for offset in range(far - 2, -1, -1):
        up = lax.ppermute(up, "z", ring(size, 1))
        down = lax.ppermute(down, "z", ring(size, -1))
        if offset:
            up = up + partial[offset]
            down = down + partial[-offset]
    return partial[0], up, down


def gather_over_z(own):
    size = lax.axis_size("z")
    far = size // 2
    cut = own.shape[0] // 2
    up, down = own, own
    parts = {0: own}
    for step in range(1, far):
        up = lax.ppermute(up, "z", ring(size, 1))
        down = lax.ppermute(down, "z", ring(size, -1))
        parts[-step], parts[step] = up, down
    up = lax.ppermute(up[:cut], "z", ring(size, 1))
    down = lax.ppermute(down[cut:], "z", ring(size, -1))
    parts[far] = jnp.concatenate([up, down])
    return parts


def gather_over_y(series):
    size = 4
    y = 2 * lax.axis_index("yh") + lax.axis_index("yl")

    def from_ahead(step):
        return [(2 * (i % 2) + i // 2, 2 * (j % 2) + j // 2)
                for j in range(size) for i in [(j + step) % size]]

    whole = jnp.zeros((2, 2, *series.shape), series.dtype)
    for step in range(size):
        part = lax.ppermute(series, ("yl", "yh"), from_ahead(step)) if step else series
        start = (lax.rem(y + step, size) // 2, step % 2, 0, 0)
        whole = lax.dynamic_update_slice(whole, part[None, None], start)
    return whole


def gather_over_x(pieces):
    size = lax.axis_size("x")
    c, x = lax.axis_index("c"), lax.axis_index("x")
    other = swap(pieces, "c")
    both = jnp.stack([jnp.where(c == 0, pieces, other), jnp.where(c == 0, other, pieces)], 2)
    both = jnp.swapaxes(both, 0, 1)
    whole = jnp.zeros((both.shape[0], size, *both.shape[1:]), both.dtype)
    for step in range(size):
        part = lax.ppermute(both, "x", ring(size, step)) if step else both
        whole = lax.dynamic_update_index_in_dim(whole, part, lax.rem(x - step + size, size), 1)
    whole = whole.reshape(both.shape[0], -1, both.shape[-1])
    return jnp.concatenate([whole[0], whole[1]], axis=1)


def reduce_over_unk(result):
    size = lax.axis_size(UNK)
    pieces = result.reshape(size, result.shape[0] // size, result.shape[1])
    return jnp.sum(lax.all_to_all(pieces, UNK, 0, 0, tiled=True), axis=0)


def on_device(signals, kernel, tap_weights):
    sensors, vectors, steps_here = signals.shape
    lags, unknowns = kernel.shape[1:]
    yl, z = lax.axis_index("yl"), lax.axis_index("z")
    z_size = lax.axis_size("z")
    slot = unknowns // (2 * z_size)
    matrix = kernel.reshape(sensors * lags, unknowns)

    sent = pairs_of(matrix, 1 - yl, z)
    pieces = gather_over_y(signals.reshape(sensors * vectors, steps_here).T)
    pieces, sent, matrix = lax.optimization_barrier((pieces, sent, matrix))
    given = [swap(block, "yl") for block in sent]
    kept = pairs_of(matrix, yl, z)
    series = gather_over_x(pieces)
    window = window_of(series, lags, vectors)
    taps = lax.dynamic_slice_in_dim(tap_weights, (yl * z_size + z) * slot, slot, 1)

    partial = {}
    for i, (low, high) in enumerate(PAIRS):
        total = adjoint_of(kept[i], given[i], window)
        for k, rows in ((low, total[:slot]), (high, total[slot:])):
            partial[k if k <= z_size // 2 else k - z_size] = rows
    smoothed = gather_over_z(smooth_of(reduce_over_z(partial), taps, vectors))

    def parts_of(pairs):
        return [smoothed[k if k <= z_size // 2 else k - z_size] for pair in pairs for k in pair]

    parts = parts_of(PAIRS[2:])
    with jax.named_scope("early_other"):
        other = early_of(given[2:], parts)
    with jax.named_scope("early_own"):
        own = early_of(kept[2:], parts)
    parts = parts_of(PAIRS[:2])
    other = forward_of(given[:2], parts, other, lags, vectors)
    own = forward_of(kept[:2], parts, own, lags, vectors)
    result = reduce_over_unk(own + swap(other, "yl"))
    return result.T.reshape(sensors, vectors, steps_here)


def solution(mesh):
    sens, unk = mesh.devices.shape
    fine = Mesh(mesh.devices.reshape(sens // 2, 2, unk // 4, 2, 2), ("z", "yl", *UNK))
    sensor_axes = ("z", "yl")
    return jax.shard_map(
        on_device,
        mesh=fine,
        in_specs=(P(sensor_axes, None, UNK), P(sensor_axes, None, UNK), P(None, UNK)),
        out_specs=P(sensor_axes, None, UNK),
        check_vma=False,
    )
```

```python
import functools

import jax
import jax.numpy as jnp
from jax import lax
from jax.experimental import pallas as pl
from jax.experimental.pallas import tpu as pltpu
from jax.sharding import Mesh, PartitionSpec as P


HIGH = lax.Precision.HIGH
UNK = ("x", "yh", "c")
PAIRS = ((4, 0), (3, 5), (2, 6), (1, 7))


def ring(size, step):
    return [(i, (i + step) % size) for i in range(size)]


def swap(value, axis):
    return lax.ppermute(value, axis, [(0, 1), (1, 0)])


def split(value):
    high = value.astype(jnp.bfloat16)
    return high, (value - high.astype(jnp.float32)).astype(jnp.bfloat16)


def mirror(steps):
    row = lax.broadcasted_iota(jnp.int32, (steps, steps), 0)
    column = lax.broadcasted_iota(jnp.int32, (steps, steps), 1)
    return jnp.where(row + column == steps - 1, 1.0, 0.0)


SUBLANES = 8


def later(tile, move, lane):
    return tile if move == 0 else jnp.where(lane >= move, pltpu.roll(tile, move, 1), 0.0)


def later_by_row(tile, lane, row):
    return jnp.where(lane >= row, pltpu.roll(tile, 0, 1, stride=1, stride_axis=0), 0.0)


def window_kernel(series_ref, window_ref, rows_ref, *, group, vectors, lags, steps):
    block = pl.program_id(0)

    @pl.when(block == 0)
    def _():
        rows_ref[...] = lax.dot_general(
            series_ref[...], mirror(steps), (((0,), (0,)), ((), ())),
            precision=lax.Precision.HIGHEST,
        )

    lane = lax.broadcasted_iota(jnp.int32, (SUBLANES, steps), 1)
    lag = lax.broadcasted_iota(jnp.int32, (SUBLANES, steps), 0)
    for s in range(group):
        for b in range(vectors):
            row = rows_ref[pl.ds((block * group + s) * vectors + b, 1), :]
            tile = later_by_row(jnp.broadcast_to(row, (SUBLANES, steps)), lane, lag)
            for move in range(0, lags, SUBLANES):
                place = s * lags + move
                window_ref[place : place + SUBLANES, b * steps : (b + 1) * steps] = later(
                    tile, move, lane
                )


def window_of(series, lags, vectors):
    steps, columns = series.shape
    sensors = columns // vectors
    group = 4
    return pl.pallas_call(
        functools.partial(
            window_kernel, group=group, vectors=vectors, lags=lags, steps=steps
        ),
        grid=(sensors // group,),
        out_shape=jax.ShapeDtypeStruct((sensors * lags, vectors * steps), jnp.float32),
        in_specs=[pl.BlockSpec((steps, columns), lambda i: (0, 0))],
        out_specs=pl.BlockSpec((group * lags, vectors * steps), lambda i: (i, 0)),
        scratch_shapes=[pltpu.VMEM((columns, steps), jnp.float32)],
        name="window",
    )(series)


def pair_kernel(scalars_ref, kernel_ref, *out_refs, lanes):
    z = scalars_ref[1]
    slots = 2 * len(PAIRS)
    slot = lanes // 2
    lane = lax.broadcasted_iota(jnp.int32, (kernel_ref.shape[0], lanes), 1)

    def half_of(offset, high):
        place = lax.rem(z + offset, slots)
        start = pl.multiple_of(place // 2 * lanes, lanes)
        shift = lax.rem(lax.rem(place, 2) + high, 2) * slot
        return pltpu.roll(kernel_ref[:, pl.ds(start, lanes)], shift, 1)

    pairs = iter(PAIRS)
    for out_ref in out_refs:
        for start in range(0, out_ref.shape[1], lanes):
            low, high = next(pairs)
            out_ref[:, start : start + lanes] = jnp.where(
                lane < slot, half_of(low, 0), half_of(high, 1)
            )


def pairs_of(matrix, half, z, outputs):
    rows, unknowns = matrix.shape
    width = unknowns // 2
    block = rows // 4
    return pl.pallas_call(
        functools.partial(pair_kernel, lanes=width // len(PAIRS)),
        grid_spec=pltpu.PrefetchScalarGridSpec(
            num_scalar_prefetch=1,
            grid=(rows // block,),
            in_specs=[pl.BlockSpec((block, width), lambda i, scalars: (i, scalars[0]))],
            out_specs=[
                pl.BlockSpec((block, width // outputs), lambda i, scalars: (i, 0))
            ] * outputs,
        ),
        out_shape=[jax.ShapeDtypeStruct((rows, width // outputs), jnp.float32)] * outputs,
        name="pairs",
    )(jnp.stack([half, z]).astype(jnp.int32), matrix)


def three_pass(high, low, right_high, right_low):
    dot = functools.partial(jnp.dot, preferred_element_type=jnp.float32)
    rows = high.shape[0]
    both = dot(jnp.concatenate([high, low]), right_high)
    return both[:rows] + both[rows:] + dot(high, right_low)


def fill(high_ref, low_ref, parts):
    start = 0
    for part in parts:
        here = slice(start, start + part.shape[0])
        high_ref[here, :], low_ref[here, :] = split(part[...])
        start += part.shape[0]


def forward_kernel(*refs, parts, group, vectors, lags, steps):
    before_ref, out_ref, high_ref, low_ref, product_ref, rows_ref = refs[-6:]
    step = pl.program_id(0)

    @pl.when(step == 0)
    def _():
        fill(high_ref, low_ref, refs[:parts])
        product_ref[1] = jnp.zeros(product_ref.shape[1:], jnp.float32)

    lane = lax.broadcasted_iota(jnp.int32, (SUBLANES, steps), 1)
    lag = lax.broadcasted_iota(jnp.int32, (SUBLANES, steps), 0)
    block = jnp.maximum(step - 1, 0)
    ready = lax.rem(step + 1, 2)
    for s in range(group):
        for b in range(vectors):
            total = None
            for move in range(0, lags, SUBLANES):
                place = s * lags + move
                tile = product_ref[
                    ready, place : place + SUBLANES, b * steps : (b + 1) * steps
                ]
                tile = later(tile, move, lane)
                total = tile if total is None else total + tile
            rows_ref[pl.ds((block * group + s) * vectors + b, 1), :] = jnp.sum(
                later_by_row(total, lane, lag), axis=0, keepdims=True
            )
    high, low = split(jnp.concatenate([ref[...] for ref in refs[parts:-6]], axis=1))
    product_ref[lax.rem(step, 2)] = before_ref[...] + three_pass(
        high, low, high_ref[...], low_ref[...]
    )

    @pl.when(step == pl.num_programs(0) - 1)
    def _():
        out_ref[...] = rows_ref[...].T


def forward_of(kernels, parts, before, lags, vectors):
    rows, columns = before.shape
    width = sum(kernel.shape[1] for kernel in kernels)
    steps = columns // vectors
    sensors = rows // lags
    group = 8
    last = sensors // group - 1

    def block_of(i):
        return (jnp.minimum(i, last), 0)

    return pl.pallas_call(
        functools.partial(
            forward_kernel, parts=len(parts), group=group, vectors=vectors, lags=lags, steps=steps
        ),
        grid=(last + 2,),
        out_shape=jax.ShapeDtypeStruct((steps, sensors * vectors), jnp.float32),
        in_specs=[pl.BlockSpec(part.shape, lambda i: (0, 0)) for part in parts]
        + [pl.BlockSpec((group * lags, kernel.shape[1]), block_of) for kernel in kernels]
        + [pl.BlockSpec((group * lags, columns), block_of)],
        out_specs=pl.BlockSpec((steps, sensors * vectors), lambda i: (0, 0)),
        scratch_shapes=[
            pltpu.VMEM((width, columns), jnp.bfloat16),
            pltpu.VMEM((width, columns), jnp.bfloat16),
            pltpu.VMEM((2, group * lags, columns), jnp.float32),
            pltpu.VMEM((sensors * vectors, steps), jnp.float32),
        ],
        name="forward",
    )(*parts, *kernels, before)


def smooth_kernel(own_ref, up_ref, down_ref, taps_ref, out_ref, *, vectors, steps):
    taps, rows = taps_ref.shape
    half = (taps - 1) // 2
    weights = taps_ref[...].T
    turn = mirror(steps)
    lane = lax.broadcasted_iota(jnp.int32, (rows, steps), 1)
    for b in range(vectors):
        here = (slice(None), slice(b * steps, (b + 1) * steps))
        block = jnp.dot(
            own_ref[here] + up_ref[here] + down_ref[here], turn, precision=lax.Precision.HIGHEST
        )
        total = weights[:, half : half + 1] * block
        for k in range(taps):
            move = k - half
            if move == 0:
                continue
            moved = pltpu.roll(block, (-move) % steps, 1)
            inside = lane < steps - move if move > 0 else lane >= -move
            total = total + weights[:, k : k + 1] * jnp.where(inside, moved, 0.0)
        out_ref[:, b * steps : (b + 1) * steps] = total


def smooth_of(addends, taps, vectors):
    columns = addends[0].shape[1]
    return pl.pallas_call(
        functools.partial(smooth_kernel, vectors=vectors, steps=columns // vectors),
        out_shape=jax.ShapeDtypeStruct(addends[0].shape, jnp.float32),
        in_specs=[pl.BlockSpec(memory_space=pltpu.VMEM)] * 4,
        out_specs=pl.BlockSpec(memory_space=pltpu.VMEM),
        name="smooth",
    )(*addends, taps)


def send_z(value, step):
    return lax.ppermute(value, "z", ring(lax.axis_size("z"), step))


def reduce_over_z(addend_of):
    far = lax.axis_size("z") // 2
    value = addend_of(far)
    cut = value.shape[0] // 2
    up = send_z(value[:cut], 1)
    down = send_z(value[cut:], -1)
    above, below = addend_of(far - 1), addend_of(1 - far)
    up = jnp.concatenate([above[:cut] + up, above[cut:]])
    down = jnp.concatenate([below[:cut], below[cut:] + down])
    for offset in range(far - 2, -1, -1):
        up = send_z(up, 1)
        down = send_z(down, -1)
        if offset:
            up = up + addend_of(offset)
            down = down + addend_of(-offset)
    return addend_of(0), up, down


def gather_over_z(own):
    far = lax.axis_size("z") // 2
    cut = own.shape[0] // 2
    up, down = own, own
    parts = {0: own}
    for step in range(1, far):
        up = send_z(up, 1)
        down = send_z(down, -1)
        parts[-step], parts[step] = up, down
    up = send_z(up[:cut], 1)
    down = send_z(down[cut:], -1)
    parts[far] = jnp.concatenate([up, down])
    return parts


def gather_over_y(series):
    size = 4
    y = 2 * lax.axis_index("yh") + lax.axis_index("yl")

    def from_ahead(step):
        return [(2 * (i % 2) + i // 2, 2 * (j % 2) + j // 2)
                for j in range(size) for i in [(j + step) % size]]

    whole = jnp.zeros((2, 2, *series.shape), series.dtype)
    for step in range(size):
        part = lax.ppermute(series, ("yl", "yh"), from_ahead(step)) if step else series
        start = (lax.rem(y + step, size) // 2, step % 2, 0, 0)
        whole = lax.dynamic_update_slice(whole, part[None, None], start)
    return whole


def gather_over_x(pieces):
    size = lax.axis_size("x")
    c, x = lax.axis_index("c"), lax.axis_index("x")
    other = swap(pieces, "c")
    both = jnp.stack([jnp.where(c == 0, pieces, other), jnp.where(c == 0, other, pieces)], 2)
    both = jnp.swapaxes(both, 0, 1)
    whole = jnp.zeros((both.shape[0], size, *both.shape[1:]), both.dtype)
    for step in range(size):
        part = lax.ppermute(both, "x", ring(size, step)) if step else both
        whole = lax.dynamic_update_index_in_dim(whole, part, lax.rem(x - step + size, size), 1)
    return whole.reshape(both.shape[0], -1, both.shape[-1])


def reduce_over_unk(result):
    size = lax.axis_size(UNK)
    pieces = result.reshape(size, result.shape[0] // size, result.shape[1])
    return jnp.sum(lax.all_to_all(pieces, UNK, 0, 0, tiled=True), axis=0)


def action(signals, kernel, tap_weights):
    sensors, vectors, steps_here = signals.shape
    lags, unknowns = kernel.shape[1:]
    yl, z = lax.axis_index("yl"), lax.axis_index("z")
    z_size = lax.axis_size("z")
    slot = unknowns // (2 * z_size)
    matrix = kernel.reshape(sensors * lags, unknowns)

    def correlate(block, window):
        return lax.dot_general(block, window, (((0,), (0,)), ((), ())), precision=HIGH)

    sent = pairs_of(matrix, 1 - yl, z, len(PAIRS))
    pieces = gather_over_y(signals.reshape(sensors * vectors, steps_here).T)
    pieces, sent, matrix = lax.optimization_barrier((pieces, sent, matrix))
    given = []
    for block in sent:
        given.append(swap(block, "yl"))
    kept = pairs_of(matrix, yl, z, 2)
    series = gather_over_x(pieces)
    own_window = window_of(series[0], lags, vectors)
    other_window = window_of(series[1], lags, vectors)
    taps = lax.dynamic_slice_in_dim(tap_weights, (yl * z_size + z) * slot, slot, 1)

    addends = {}
    for i, pair in enumerate(PAIRS):
        if i % 2 == 0:
            mine = correlate(kept[i // 2], own_window)
        first = i % 2 * 2 * slot
        total = mine[first : first + 2 * slot] + correlate(given[i], other_window)
        for j, k in enumerate(pair):
            addends[k] = total[j * slot : (j + 1) * slot]
    addends = smooth_of(reduce_over_z(lambda k: addends[k % z_size]), taps, vectors)
    smoothed = gather_over_z(addends)

    def parts_of(pairs):
        return [smoothed[k if k <= z_size // 2 else k - z_size] for pair in pairs for k in pair]

    parts = parts_of(PAIRS[2:])
    whole = jnp.concatenate(parts)
    other = jnp.dot(jnp.concatenate(given[2:], 1), whole, precision=HIGH)
    own = jnp.dot(kept[1], whole, precision=HIGH)
    parts = parts_of(PAIRS[:2])
    other = forward_of(given[:2], parts, other, lags, vectors)
    own = forward_of(kept[:1], parts, own, lags, vectors)
    result = reduce_over_unk(own + swap(other, "yl"))
    return result.T.reshape(sensors, vectors, steps_here)


def solution(mesh):
    sens, unk = mesh.devices.shape
    fine = Mesh(mesh.devices.reshape(sens // 2, 2, unk // 4, 2, 2), ("z", "yl", *UNK))
    sensor_axes = ("z", "yl")
    return jax.shard_map(
        action,
        mesh=fine,
        in_specs=(P(sensor_axes, None, UNK), P(sensor_axes, None, UNK), P(None, UNK)),
        out_specs=P(sensor_axes, None, UNK),
        check_vma=False,
    )
```

```python
import functools

import jax
import jax.numpy as jnp
from jax import lax
from jax.experimental import pallas as pl
from jax.experimental.pallas import tpu as pltpu
from jax.sharding import Mesh, PartitionSpec as P


HIGH = lax.Precision.HIGH
UNK = ("x", "yh", "c")
PAIRS = ((4, 0), (3, 5), (2, 6), (1, 7))


def ring(size, step):
    return [(i, (i + step) % size) for i in range(size)]


def swap(value, axis):
    return lax.ppermute(value, axis, [(0, 1), (1, 0)])


def split(value):
    high = value.astype(jnp.bfloat16)
    return high, (value - high.astype(jnp.float32)).astype(jnp.bfloat16)


def mirror(steps):
    row = lax.broadcasted_iota(jnp.int32, (steps, steps), 0)
    column = lax.broadcasted_iota(jnp.int32, (steps, steps), 1)
    return jnp.where(row + column == steps - 1, 1.0, 0.0)


VMEM = pl.BlockSpec(memory_space=pltpu.VMEM)


def room(mebibytes):
    return pltpu.CompilerParams(vmem_limit_bytes=mebibytes * 2**20)


def resident(value):
    return pltpu.with_memory_space_constraint(value, pltpu.VMEM)


def skewed(tile):
    lane = lax.broadcasted_iota(jnp.int32, tile.shape, 1)
    row = lax.broadcasted_iota(jnp.int32, tile.shape, 0)
    return jnp.where(lane >= row, pltpu.roll(tile, 0, 1, stride=1, stride_axis=0), 0.0)


def window_kernel(series_ref, window_ref, rows_ref, *, group, vectors, lags, steps):
    rows_ref[...] = lax.dot_general(
        series_ref[...], mirror(steps), (((0,), (0,)), ((), ())),
        precision=lax.Precision.HIGHEST,
    )

    def body(block, carry):
        for s in range(group):
            sensor = block * group + s
            for b in range(vectors):
                row = rows_ref[pl.ds(sensor * vectors + b, 1), :]
                here = pl.ds(pl.multiple_of(sensor * lags, lags), lags)
                window_ref[here, b * steps : (b + 1) * steps] = skewed(
                    jnp.broadcast_to(row, (lags, steps))
                )
        return carry

    lax.fori_loop(0, rows_ref.shape[0] // (vectors * group), body, 0)


def window_of(series, lags, vectors):
    steps, columns = series.shape
    sensors = columns // vectors
    return pl.pallas_call(
        functools.partial(window_kernel, group=4, vectors=vectors, lags=lags, steps=steps),
        out_shape=pltpu.VMEM((sensors * lags, vectors * steps), jnp.float32),
        in_specs=[VMEM],
        out_specs=VMEM,
        scratch_shapes=[pltpu.VMEM((columns, steps), jnp.float32)],
        compiler_params=room(4),
        name="window",
    )(resident(series))


def pair_kernel(scalars_ref, kernel_ref, *out_refs, lanes):
    half, z = scalars_ref[0], scalars_ref[1]
    slots = 2 * len(PAIRS)
    slot = lanes // 2
    block = 128
    lane = lax.broadcasted_iota(jnp.int32, (block, lanes), 1)

    def body(i, carry):
        here = pl.ds(pl.multiple_of(i * block, block), block)

        def half_of(offset, high):
            place = lax.rem(z + offset, slots)
            start = pl.multiple_of((half * len(PAIRS) + place // 2) * lanes, lanes)
            shift = lax.rem(lax.rem(place, 2) + high, 2) * slot
            return pltpu.roll(kernel_ref[here, pl.ds(start, lanes)], shift, 1)

        pairs = iter(PAIRS)
        for out_ref in out_refs:
            for start in range(0, out_ref.shape[1], lanes):
                low, high = next(pairs)
                out_ref[here, start : start + lanes] = jnp.where(
                    lane < slot, half_of(low, 0), half_of(high, 1)
                )
        return carry

    lax.fori_loop(0, kernel_ref.shape[0] // block, body, 0)


def pairs_of(matrix, half, z, outputs):
    rows, unknowns = matrix.shape
    width = unknowns // 2
    return pl.pallas_call(
        functools.partial(pair_kernel, lanes=width // len(PAIRS)),
        out_shape=[pltpu.VMEM((rows, width // outputs), jnp.float32)] * outputs,
        in_specs=[pl.BlockSpec(memory_space=pltpu.SMEM), VMEM],
        out_specs=[VMEM] * outputs,
        compiler_params=room(4),
        name="pairs",
    )(jnp.stack([half, z]).astype(jnp.int32), matrix)


def three_pass(high, low, right_high, right_low):
    dot = functools.partial(jnp.dot, preferred_element_type=jnp.float32)
    rows = high.shape[0]
    both = dot(jnp.concatenate([high, low]), right_high)
    return both[:rows] + both[rows:] + dot(high, right_low)


def fill(high_ref, low_ref, parts):
    start = 0
    for part in parts:
        here = slice(start, start + part.shape[0])
        high_ref[here, :], low_ref[here, :] = split(part[...])
        start += part.shape[0]


def forward_kernel(*refs, parts, group, vectors, lags, steps):
    before_ref, out_ref, high_ref, low_ref, product_ref, rows_ref = refs[-6:]
    blocks = before_ref.shape[0] // (group * lags)
    fill(high_ref, low_ref, refs[:parts])

    def multiply(block):
        here = pl.ds(pl.multiple_of(block * group * lags, group * lags), group * lags)
        high, low = split(jnp.concatenate([ref[here, :] for ref in refs[parts:-6]], axis=1))
        product_ref[lax.rem(block, 2)] = before_ref[here, :] + three_pass(
            high, low, high_ref[...], low_ref[...]
        )

    def shear(block):
        for s in range(group):
            for b in range(vectors):
                tile = product_ref[
                    lax.rem(block, 2), s * lags : (s + 1) * lags, b * steps : (b + 1) * steps
                ]
                rows_ref[pl.ds((block * group + s) * vectors + b, 1), :] = jnp.sum(
                    skewed(tile), axis=0, keepdims=True
                )

    multiply(0)

    def body(block, carry):
        shear(block - 1)
        multiply(block)
        return carry

    lax.fori_loop(1, blocks, body, 0)
    shear(blocks - 1)
    out_ref[...] = rows_ref[...].T


def forward_of(kernels, parts, before, lags, vectors):
    rows, columns = before.shape
    width = sum(kernel.shape[1] for kernel in kernels)
    steps = columns // vectors
    sensors = rows // lags
    group = 8
    operands = [resident(value) for value in (*parts, *kernels, before)]
    return pl.pallas_call(
        functools.partial(
            forward_kernel, parts=len(parts), group=group, vectors=vectors, lags=lags, steps=steps
        ),
        out_shape=pltpu.VMEM((steps, sensors * vectors), jnp.float32),
        in_specs=[VMEM] * len(operands),
        out_specs=VMEM,
        scratch_shapes=[
            pltpu.VMEM((width, columns), jnp.bfloat16),
            pltpu.VMEM((width, columns), jnp.bfloat16),
            pltpu.VMEM((2, group * lags, columns), jnp.float32),
            pltpu.VMEM((sensors * vectors, steps), jnp.float32),
        ],
        compiler_params=room(12),
        name="forward",
    )(*operands)


def smooth_kernel(own_ref, up_ref, down_ref, taps_ref, out_ref, *, vectors, steps):
    taps, rows = taps_ref.shape
    half = (taps - 1) // 2
    weights = taps_ref[...].T
    turn = mirror(steps)
    lane = lax.broadcasted_iota(jnp.int32, (rows, steps), 1)
    for b in range(vectors):
        here = (slice(None), slice(b * steps, (b + 1) * steps))
        block = jnp.dot(
            own_ref[here] + up_ref[here] + down_ref[here], turn, precision=lax.Precision.HIGHEST
        )
        total = weights[:, half : half + 1] * block
        for k in range(taps):
            move = k - half
            if move == 0:
                continue
            moved = pltpu.roll(block, (-move) % steps, 1)
            inside = lane < steps - move if move > 0 else lane >= -move
            total = total + weights[:, k : k + 1] * jnp.where(inside, moved, 0.0)
        out_ref[:, b * steps : (b + 1) * steps] = total


def smooth_of(addends, taps, vectors):
    columns = addends[0].shape[1]
    return pl.pallas_call(
        functools.partial(smooth_kernel, vectors=vectors, steps=columns // vectors),
        out_shape=pltpu.VMEM(addends[0].shape, jnp.float32),
        in_specs=[VMEM] * 4,
        out_specs=VMEM,
        compiler_params=room(4),
        name="smooth",
    )(*(resident(value) for value in (*addends, taps)))


def send_z(value, step):
    return lax.ppermute(value, "z", ring(lax.axis_size("z"), step))


def reduce_over_z(addend_of):
    far = lax.axis_size("z") // 2
    value = addend_of(far)
    cut = value.shape[0] // 2
    up = send_z(value[:cut], 1)
    down = send_z(value[cut:], -1)
    above, below = addend_of(far - 1), addend_of(1 - far)
    up = jnp.concatenate([above[:cut] + up, above[cut:]])
    down = jnp.concatenate([below[:cut], below[cut:] + down])
    for offset in range(far - 2, -1, -1):
        up = send_z(up, 1)
        down = send_z(down, -1)
        if offset:
            up = up + addend_of(offset)
            down = down + addend_of(-offset)
    return addend_of(0), up, down


def gather_over_z(own):
    far = lax.axis_size("z") // 2
    cut = own.shape[0] // 2
    up, down = own, own
    parts = {0: own}
    for step in range(1, far):
        up = send_z(up, 1)
        down = send_z(down, -1)
        parts[-step], parts[step] = up, down
    up = send_z(up[:cut], 1)
    down = send_z(down[cut:], -1)
    parts[far] = jnp.concatenate([up, down])
    return parts


def gather_over_y(series):
    size = 4
    y = 2 * lax.axis_index("yh") + lax.axis_index("yl")

    def from_ahead(step):
        return [(2 * (i % 2) + i // 2, 2 * (j % 2) + j // 2)
                for j in range(size) for i in [(j + step) % size]]

    whole = jnp.zeros((2, 2, *series.shape), series.dtype)
    for step in range(size):
        part = lax.ppermute(series, ("yl", "yh"), from_ahead(step)) if step else series
        start = (lax.rem(y + step, size) // 2, step % 2, 0, 0)
        whole = lax.dynamic_update_slice(whole, part[None, None], start)
    return whole


def gather_over_x(pieces):
    size = lax.axis_size("x")
    c, x = lax.axis_index("c"), lax.axis_index("x")
    other = swap(pieces, "c")
    both = jnp.stack([jnp.where(c == 0, pieces, other), jnp.where(c == 0, other, pieces)], 2)
    both = jnp.swapaxes(both, 0, 1)
    whole = jnp.zeros((both.shape[0], size, *both.shape[1:]), both.dtype)
    for step in range(size):
        part = lax.ppermute(both, "x", ring(size, step)) if step else both
        whole = lax.dynamic_update_index_in_dim(whole, part, lax.rem(x - step + size, size), 1)
    return whole.reshape(both.shape[0], -1, both.shape[-1])


def reduce_over_unk(result):
    size = lax.axis_size(UNK)
    pieces = result.reshape(size, result.shape[0] // size, result.shape[1])
    return jnp.sum(lax.all_to_all(pieces, UNK, 0, 0, tiled=True), axis=0)


def action(signals, kernel, tap_weights):
    sensors, vectors, steps_here = signals.shape
    lags, unknowns = kernel.shape[1:]
    yl, z = lax.axis_index("yl"), lax.axis_index("z")
    z_size = lax.axis_size("z")
    slot = unknowns // (2 * z_size)
    matrix = resident(kernel.reshape(sensors * lags, unknowns))

    def correlate(block, window):
        return lax.dot_general(block, window, (((0,), (0,)), ((), ())), precision=HIGH)

    sent = pairs_of(matrix, 1 - yl, z, len(PAIRS))
    pieces = gather_over_y(signals.reshape(sensors * vectors, steps_here).T)
    pieces, sent, matrix = lax.optimization_barrier((pieces, sent, matrix))
    given = []
    for block in sent:
        given.append(swap(block, "yl"))
    kept = pairs_of(matrix, yl, z, 2)
    series = gather_over_x(pieces)
    own_window = window_of(series[0], lags, vectors)
    other_window = window_of(series[1], lags, vectors)
    taps = lax.dynamic_slice_in_dim(tap_weights, (yl * z_size + z) * slot, slot, 1)

    addends = {}
    for i, pair in enumerate(PAIRS):
        if i % 2 == 0:
            mine = correlate(kept[i // 2], own_window)
        first = i % 2 * 2 * slot
        total = mine[first : first + 2 * slot] + correlate(given[i], other_window)
        for j, k in enumerate(pair):
            addends[k] = total[j * slot : (j + 1) * slot]
    addends = smooth_of(reduce_over_z(lambda k: addends[k % z_size]), taps, vectors)
    smoothed = gather_over_z(addends)

    def parts_of(pairs):
        return [smoothed[k if k <= z_size // 2 else k - z_size] for pair in pairs for k in pair]

    parts = parts_of(PAIRS[2:])
    whole = jnp.concatenate(parts)
    other = jnp.dot(jnp.concatenate(given[2:], 1), whole, precision=HIGH)
    own = jnp.dot(kept[1], whole, precision=HIGH)
    parts = parts_of(PAIRS[:2])
    other = forward_of(given[:2], parts, other, lags, vectors)
    own = forward_of(kept[:1], parts, own, lags, vectors)
    result = reduce_over_unk(own + swap(other, "yl"))
    return result.T.reshape(sensors, vectors, steps_here)


def solution(mesh):
    sens, unk = mesh.devices.shape
    fine = Mesh(mesh.devices.reshape(sens // 2, 2, unk // 4, 2, 2), ("z", "yl", *UNK))
    sensor_axes = ("z", "yl")
    return jax.shard_map(
        action,
        mesh=fine,
        in_specs=(P(sensor_axes, None, UNK), P(sensor_axes, None, UNK), P(None, UNK)),
        out_specs=P(sensor_axes, None, UNK),
        check_vma=False,
    )
```

```python
import functools

import jax
import jax.numpy as jnp
from jax import lax
from jax.experimental import pallas as pl
from jax.experimental.pallas import tpu as pltpu
from jax.sharding import Mesh, PartitionSpec as P


UNK = ("x", "yh", "c")
PAIRS = ((4, 0), (3, 5), (2, 6), (1, 7))


def ring(size, step):
    return [(i, (i + step) % size) for i in range(size)]


def swap(value, axis):
    return lax.ppermute(value, axis, [(0, 1), (1, 0)])


def split(value):
    high = value.astype(jnp.bfloat16)
    return high, (value - high.astype(jnp.float32)).astype(jnp.bfloat16)


def mirror(steps):
    row = lax.broadcasted_iota(jnp.int32, (steps, steps), 0)
    column = lax.broadcasted_iota(jnp.int32, (steps, steps), 1)
    return jnp.where(row + column == steps - 1, 1.0, 0.0)


VMEM = pl.BlockSpec(memory_space=pltpu.VMEM)


def room(mebibytes):
    return pltpu.CompilerParams(vmem_limit_bytes=mebibytes * 2**20)


def resident(value):
    return pltpu.with_memory_space_constraint(value, pltpu.VMEM)


def skewed(tile):
    lane = lax.broadcasted_iota(jnp.int32, tile.shape, 1)
    row = lax.broadcasted_iota(jnp.int32, tile.shape, 0)
    return jnp.where(lane >= row, pltpu.roll(tile, 0, 1, stride=1, stride_axis=0), 0.0)


def window_kernel(series_ref, high_ref, low_ref, rows_ref, *, group, vectors, lags, steps):
    rows_ref[...] = lax.dot_general(
        series_ref[...], mirror(steps), (((0,), (0,)), ((), ())),
        precision=lax.Precision.HIGHEST,
    )

    def body(block, carry):
        for s in range(group):
            sensor = block * group + s
            for b in range(vectors):
                row = rows_ref[pl.ds(sensor * vectors + b, 1), :]
                here = pl.ds(pl.multiple_of(sensor * lags, lags), lags)
                place = (here, slice(b * steps, (b + 1) * steps))
                high_ref[place], low_ref[place] = split(
                    skewed(jnp.broadcast_to(row, (lags, steps)))
                )
        return carry

    lax.fori_loop(0, rows_ref.shape[0] // (vectors * group), body, 0)


def window_of(series, lags, vectors):
    steps, columns = series.shape
    sensors = columns // vectors
    return pl.pallas_call(
        functools.partial(window_kernel, group=4, vectors=vectors, lags=lags, steps=steps),
        out_shape=[pltpu.VMEM((sensors * lags, vectors * steps), jnp.bfloat16)] * 2,
        in_specs=[VMEM],
        out_specs=[VMEM] * 2,
        scratch_shapes=[pltpu.VMEM((columns, steps), jnp.float32)],
        compiler_params=room(4),
        name="window",
    )(resident(series))


def pair_kernel(scalars_ref, kernel_ref, *refs, lanes):
    *out_refs, half_ref, arrived = refs
    half, z = scalars_ref[0], scalars_ref[1]
    slots = 2 * len(PAIRS)
    slot = lanes // 2
    rows, width = half_ref.shape
    blocks = arrived.shape[0]
    block = rows // blocks
    columns = pl.ds(pl.multiple_of(half * width, width), width)

    def copy_of(i):
        here = pl.ds(pl.multiple_of(i * block, block), block)
        return pltpu.make_async_copy(
            kernel_ref.at[here, columns], half_ref.at[here, :], arrived.at[i]
        )

    for i in range(blocks):
        copy_of(i).start()
    lane = lax.broadcasted_iota(jnp.int32, (block, lanes), 1)

    def body(i, carry):
        copy_of(i).wait()
        here = pl.ds(pl.multiple_of(i * block, block), block)

        def half_of(offset, high):
            place = lax.rem(z + offset, slots)
            start = pl.multiple_of(place // 2 * lanes, lanes)
            shift = lax.rem(lax.rem(place, 2) + high, 2) * slot
            return pltpu.roll(half_ref[here, pl.ds(start, lanes)], shift, 1)

        pairs = iter(PAIRS)
        for out_ref in out_refs:
            for start in range(0, out_ref.shape[1], lanes):
                low, high = next(pairs)
                out_ref[here, start : start + lanes] = jnp.where(
                    lane < slot, half_of(low, 0), half_of(high, 1)
                )
        return carry

    lax.fori_loop(0, blocks, body, 0)


def pairs_of(matrix, half, z, outputs):
    rows, unknowns = matrix.shape
    width = unknowns // 2
    blocks = 8
    return pl.pallas_call(
        functools.partial(pair_kernel, lanes=width // len(PAIRS)),
        out_shape=[pltpu.VMEM((rows, width // outputs), jnp.float32)] * outputs,
        in_specs=[
            pl.BlockSpec(memory_space=pltpu.SMEM),
            pl.BlockSpec(memory_space=pltpu.HBM),
        ],
        out_specs=[VMEM] * outputs,
        scratch_shapes=[
            pltpu.VMEM((rows, width), jnp.float32),
            pltpu.SemaphoreType.DMA((blocks,)),
        ],
        compiler_params=room(4),
        name="pairs",
    )(
        jnp.stack([half, z]).astype(jnp.int32),
        pltpu.with_memory_space_constraint(matrix, pltpu.HBM),
    )


def three_pass(high, low, right_high, right_low):
    dot = functools.partial(jnp.dot, preferred_element_type=jnp.float32)
    rows = high.shape[0]
    both = dot(jnp.concatenate([high, low]), right_high)
    return both[:rows] + both[rows:] + dot(high, right_low)


def adjoint_kernel(
    kept_ref, given_ref, kept_high_ref, kept_low_ref, given_high_ref, given_low_ref, out_ref,
    *, first, block,
):
    out_ref[...] = jnp.zeros(out_ref.shape, jnp.float32)
    width = given_ref.shape[1]

    def body(i, carry):
        here = pl.ds(pl.multiple_of(i * block, block), block)
        kept = split(kept_ref[here, first : first + width].T)
        given = split(given_ref[here, :].T)
        out_ref[...] += three_pass(
            *kept, kept_high_ref[here, :], kept_low_ref[here, :]
        ) + three_pass(*given, given_high_ref[here, :], given_low_ref[here, :])
        return carry

    lax.fori_loop(0, given_ref.shape[0] // block, body, 0)


def adjoint_of(kept, first, given, own_window, other_window):
    operands = [resident(value) for value in (kept, given, *own_window, *other_window)]
    return pl.pallas_call(
        functools.partial(adjoint_kernel, first=first, block=256),
        out_shape=pltpu.VMEM((given.shape[1], own_window[0].shape[1]), jnp.float32),
        in_specs=[VMEM] * len(operands),
        out_specs=VMEM,
        compiler_params=room(8),
        name="adjoint",
    )(*operands)


def early_kernel(*refs, parts):
    out_ref, high_ref, low_ref = refs[-3:]
    fill(high_ref, low_ref, refs[:parts])
    block = 256

    def body(i, carry):
        here = pl.ds(pl.multiple_of(i * block, block), block)
        high, low = split(jnp.concatenate([ref[here, :] for ref in refs[parts:-3]], axis=1))
        out_ref[here, :] = three_pass(high, low, high_ref[...], low_ref[...])
        return carry

    lax.fori_loop(0, out_ref.shape[0] // block, body, 0)


def early_of(kernels, parts):
    width = sum(kernel.shape[1] for kernel in kernels)
    columns = parts[0].shape[1]
    operands = [resident(value) for value in (*parts, *kernels)]
    return pl.pallas_call(
        functools.partial(early_kernel, parts=len(parts)),
        out_shape=pltpu.VMEM((kernels[0].shape[0], columns), jnp.float32),
        in_specs=[VMEM] * len(operands),
        out_specs=VMEM,
        scratch_shapes=[pltpu.VMEM((width, columns), jnp.bfloat16)] * 2,
        compiler_params=room(8),
        name="early",
    )(*operands)


def fill(high_ref, low_ref, parts):
    start = 0
    for part in parts:
        here = slice(start, start + part.shape[0])
        high_ref[here, :], low_ref[here, :] = split(part[...])
        start += part.shape[0]


def forward_kernel(*refs, parts, group, vectors, lags, steps):
    before_ref, out_ref, high_ref, low_ref, product_ref, rows_ref = refs[-6:]
    blocks = before_ref.shape[0] // (group * lags)
    fill(high_ref, low_ref, refs[:parts])

    def multiply(block):
        here = pl.ds(pl.multiple_of(block * group * lags, group * lags), group * lags)
        high, low = split(jnp.concatenate([ref[here, :] for ref in refs[parts:-6]], axis=1))
        product_ref[lax.rem(block, 2)] = before_ref[here, :] + three_pass(
            high, low, high_ref[...], low_ref[...]
        )

    def shear(block):
        for s in range(group):
            for b in range(vectors):
                tile = product_ref[
                    lax.rem(block, 2), s * lags : (s + 1) * lags, b * steps : (b + 1) * steps
                ]
                rows_ref[pl.ds((block * group + s) * vectors + b, 1), :] = jnp.sum(
                    skewed(tile), axis=0, keepdims=True
                )

    multiply(0)

    def body(block, carry):
        shear(block - 1)
        multiply(block)
        return carry

    lax.fori_loop(1, blocks, body, 0)
    shear(blocks - 1)
    out_ref[...] = rows_ref[...].T


def forward_of(kernels, parts, before, lags, vectors):
    rows, columns = before.shape
    width = sum(kernel.shape[1] for kernel in kernels)
    steps = columns // vectors
    sensors = rows // lags
    group = 8
    operands = [resident(value) for value in (*parts, *kernels, before)]
    return pl.pallas_call(
        functools.partial(
            forward_kernel, parts=len(parts), group=group, vectors=vectors, lags=lags, steps=steps
        ),
        out_shape=pltpu.VMEM((steps, sensors * vectors), jnp.float32),
        in_specs=[VMEM] * len(operands),
        out_specs=VMEM,
        scratch_shapes=[
            pltpu.VMEM((width, columns), jnp.bfloat16),
            pltpu.VMEM((width, columns), jnp.bfloat16),
            pltpu.VMEM((2, group * lags, columns), jnp.float32),
            pltpu.VMEM((sensors * vectors, steps), jnp.float32),
        ],
        compiler_params=room(12),
        name="forward",
    )(*operands)


def smooth_kernel(own_ref, up_ref, down_ref, taps_ref, out_ref, *, vectors, steps):
    taps, rows = taps_ref.shape
    half = (taps - 1) // 2
    weights = taps_ref[...].T
    turn = mirror(steps)
    lane = lax.broadcasted_iota(jnp.int32, (rows, steps), 1)
    for b in range(vectors):
        here = (slice(None), slice(b * steps, (b + 1) * steps))
        block = jnp.dot(
            own_ref[here] + up_ref[here] + down_ref[here], turn, precision=lax.Precision.HIGHEST
        )
        total = weights[:, half : half + 1] * block
        for k in range(taps):
            move = k - half
            if move == 0:
                continue
            moved = pltpu.roll(block, (-move) % steps, 1)
            inside = lane < steps - move if move > 0 else lane >= -move
            total = total + weights[:, k : k + 1] * jnp.where(inside, moved, 0.0)
        out_ref[:, b * steps : (b + 1) * steps] = total


def smooth_of(addends, taps, vectors):
    columns = addends[0].shape[1]
    return pl.pallas_call(
        functools.partial(smooth_kernel, vectors=vectors, steps=columns // vectors),
        out_shape=pltpu.VMEM(addends[0].shape, jnp.float32),
        in_specs=[VMEM] * 4,
        out_specs=VMEM,
        compiler_params=room(4),
        name="smooth",
    )(*(resident(value) for value in (*addends, taps)))


def send_z(value, step):
    return lax.ppermute(value, "z", ring(lax.axis_size("z"), step))


def reduce_over_z(addend_of):
    far = lax.axis_size("z") // 2
    value = addend_of(far)
    cut = value.shape[0] // 2
    up = send_z(value[:cut], 1)
    down = send_z(value[cut:], -1)
    above, below = addend_of(far - 1), addend_of(1 - far)
    up = jnp.concatenate([above[:cut] + up, above[cut:]])
    down = jnp.concatenate([below[:cut], below[cut:] + down])
    for offset in range(far - 2, -1, -1):
        up = send_z(up, 1)
        down = send_z(down, -1)
        if offset:
            up = up + addend_of(offset)
            down = down + addend_of(-offset)
    return addend_of(0), up, down


def gather_over_z(own):
    far = lax.axis_size("z") // 2
    cut = own.shape[0] // 2
    up, down = own, own
    parts = {0: own}
    for step in range(1, far):
        up = send_z(up, 1)
        down = send_z(down, -1)
        parts[-step], parts[step] = up, down
    up = send_z(up[:cut], 1)
    down = send_z(down[cut:], -1)
    parts[far] = jnp.concatenate([up, down])
    return parts


def gather_over_y(series):
    both = jnp.stack([series, swap(series, "yl")])
    yh = lax.axis_index("yh")
    other = lax.ppermute(both, ("yl", "yh"), [(i, 3 - i) for i in range(4)])[::-1]
    return jnp.stack([jnp.where(yh == 0, both, other), jnp.where(yh == 0, other, both)])


def gather_over_x(pieces):
    c, x = lax.axis_index("c"), lax.axis_index("x")
    other = swap(pieces, "c")
    here = jnp.stack([jnp.where(c == 0, pieces, other), jnp.where(c == 0, other, pieces)], 2)
    here = jnp.swapaxes(here, 0, 1)
    size = lax.axis_size("x")
    other = lax.ppermute(here, "x", [(i, i ^ 1) for i in range(size)])
    low = lax.rem(x, 2) == 0
    pair = jnp.stack([jnp.where(low, here, other), jnp.where(low, other, here)], 1)
    other = lax.ppermute(pair, "x", [(i, size - 1 - i) for i in range(size)])
    low = x < 2
    whole = jnp.stack([jnp.where(low, pair, other), jnp.where(low, other, pair)], 1)
    return whole.reshape(whole.shape[0], -1, whole.shape[-1])


def reduce_over_unk(result):
    size = lax.axis_size(UNK)
    pieces = result.reshape(size, result.shape[0] // size, result.shape[1])
    return jnp.sum(lax.all_to_all(pieces, UNK, 0, 0, tiled=True), axis=0)


def action(signals, kernel, tap_weights):
    sensors, vectors, steps_here = signals.shape
    lags, unknowns = kernel.shape[1:]
    yl, z = lax.axis_index("yl"), lax.axis_index("z")
    z_size = lax.axis_size("z")
    slot = unknowns // (2 * z_size)
    matrix = kernel.reshape(sensors * lags, unknowns)

    sent = pairs_of(matrix, 1 - yl, z, len(PAIRS))
    pieces = gather_over_y(signals.reshape(sensors * vectors, steps_here).T)
    pieces, sent = lax.optimization_barrier((pieces, sent))
    given = []
    for block in sent:
        given.append(swap(block, "yl"))
    kept = pairs_of(matrix, yl, z, 2)
    series = gather_over_x(pieces)
    own_window = window_of(series[0], lags, vectors)
    other_window = window_of(series[1], lags, vectors)
    taps = lax.dynamic_slice_in_dim(tap_weights, (yl * z_size + z) * slot, slot, 1)

    addends = {}
    for i, pair in enumerate(PAIRS):
        total = adjoint_of(
            kept[i // 2], i % 2 * 2 * slot, given[i], own_window, other_window
        )
        for j, k in enumerate(pair):
            addends[k] = total[j * slot : (j + 1) * slot]
    addends = smooth_of(reduce_over_z(lambda k: addends[k % z_size]), taps, vectors)
    smoothed = gather_over_z(addends)

    def parts_of(pairs):
        return [smoothed[k if k <= z_size // 2 else k - z_size] for pair in pairs for k in pair]

    parts = parts_of(PAIRS[2:])
    other = early_of(given[2:], parts)
    own = early_of(kept[1:], parts)
    parts = parts_of(PAIRS[:2])
    other = forward_of(given[:2], parts, other, lags, vectors)
    own = forward_of(kept[:1], parts, own, lags, vectors)
    result = reduce_over_unk(own + swap(other, "yl"))
    return result.T.reshape(sensors, vectors, steps_here)


def solution(mesh):
    sens, unk = mesh.devices.shape
    fine = Mesh(mesh.devices.reshape(sens // 2, 2, unk // 4, 2, 2), ("z", "yl", *UNK))
    sensor_axes = ("z", "yl")
    return jax.shard_map(
        action,
        mesh=fine,
        in_specs=(P(sensor_axes, None, UNK), P(sensor_axes, None, UNK), P(None, UNK)),
        out_specs=P(sensor_axes, None, UNK),
        check_vma=False,
    )
```

```python
import functools

import jax
import jax.numpy as jnp
from jax import lax
from jax.experimental import pallas as pl
from jax.experimental.pallas import tpu as pltpu
from jax.sharding import Mesh, PartitionSpec as P


UNK = ("x", "yh", "c")
PAIRS = ((4, 0), (3, 5), (2, 6), (1, 7))


def ring(size, step):
    return [(i, (i + step) % size) for i in range(size)]


def swap(value, axis):
    return lax.ppermute(value, axis, [(0, 1), (1, 0)])


def split(value):
    high = value.astype(jnp.bfloat16)
    return high, (value - high.astype(jnp.float32)).astype(jnp.bfloat16)


def mirror(steps):
    row = lax.broadcasted_iota(jnp.int32, (steps, steps), 0)
    column = lax.broadcasted_iota(jnp.int32, (steps, steps), 1)
    return jnp.where(row + column == steps - 1, 1.0, 0.0)


VMEM = pl.BlockSpec(memory_space=pltpu.VMEM)


def room(mebibytes):
    return pltpu.CompilerParams(vmem_limit_bytes=mebibytes * 2**20)


def resident(value):
    return pltpu.with_memory_space_constraint(value, pltpu.VMEM)


def skewed(tile):
    lane = lax.broadcasted_iota(jnp.int32, tile.shape, 1)
    row = lax.broadcasted_iota(jnp.int32, tile.shape, 0)
    return jnp.where(lane >= row, pltpu.roll(tile, 0, 1, stride=1, stride_axis=0), 0.0)


def window_kernel(series_ref, high_ref, low_ref, rows_ref, *, group, vectors, lags, steps):
    rows_ref[...] = lax.dot_general(
        series_ref[...], mirror(steps), (((0,), (0,)), ((), ())),
        precision=lax.Precision.HIGHEST,
    )

    def body(block, carry):
        for s in range(group):
            sensor = block * group + s
            for b in range(vectors):
                row = rows_ref[pl.ds(sensor * vectors + b, 1), :]
                here = pl.ds(pl.multiple_of(sensor * lags, lags), lags)
                place = (here, slice(b * steps, (b + 1) * steps))
                high_ref[place], low_ref[place] = split(
                    skewed(jnp.broadcast_to(row, (lags, steps)))
                )
        return carry

    lax.fori_loop(0, rows_ref.shape[0] // (vectors * group), body, 0)


def window_of(series, lags, vectors):
    steps, columns = series.shape
    sensors = columns // vectors
    return pl.pallas_call(
        functools.partial(window_kernel, group=4, vectors=vectors, lags=lags, steps=steps),
        out_shape=[pltpu.VMEM((sensors * lags, vectors * steps), jnp.bfloat16)] * 2,
        in_specs=[VMEM],
        out_specs=[VMEM] * 2,
        scratch_shapes=[pltpu.VMEM((columns, steps), jnp.float32)],
        compiler_params=room(4),
        name="window",
    )(resident(series))


def pair_kernel(place_ref, kernel_ref, *refs, pairs, lanes, other):
    *out_refs, half_ref, arrived = refs
    half, z = place_ref[0], place_ref[1]
    half = 1 - half if other else half
    slots = 2 * len(PAIRS)
    slot = lanes // 2
    rows, width = half_ref.shape
    blocks = arrived.shape[0]
    block = rows // blocks
    columns = pl.ds(pl.multiple_of(half * width, width), width)

    def copy_of(i):
        here = pl.ds(pl.multiple_of(i * block, block), block)
        return pltpu.make_async_copy(
            kernel_ref.at[here, columns], half_ref.at[here, :], arrived.at[i]
        )

    for i in range(blocks):
        copy_of(i).start()
    lane = lax.broadcasted_iota(jnp.int32, (block, lanes), 1)

    def body(i, carry):
        copy_of(i).wait()
        here = pl.ds(pl.multiple_of(i * block, block), block)

        def half_of(offset, high):
            place = lax.rem(z + offset, slots)
            start = pl.multiple_of(place // 2 * lanes, lanes)
            shift = lax.rem(lax.rem(place, 2) + high, 2) * slot
            return pltpu.roll(half_ref[here, pl.ds(start, lanes)], shift, 1)

        left = iter(pairs)
        for out_ref in out_refs:
            for start in range(0, out_ref.shape[1], lanes):
                low, high = next(left)
                out_ref[here, start : start + lanes] = jnp.where(
                    lane < slot, half_of(low, 0), half_of(high, 1)
                )
        return carry

    lax.fori_loop(0, blocks, body, 0)


def pairs_of(matrix, place, other, pairs, outputs):
    rows, unknowns = matrix.shape
    width = unknowns // 2
    lanes = width // len(PAIRS)
    blocks = 8
    return pl.pallas_call(
        functools.partial(pair_kernel, pairs=pairs, lanes=lanes, other=other),
        out_shape=[pltpu.VMEM((rows, lanes * len(pairs) // outputs), jnp.float32)] * outputs,
        in_specs=[
            pl.BlockSpec(memory_space=pltpu.SMEM),
            pl.BlockSpec(memory_space=pltpu.HBM),
        ],
        out_specs=[VMEM] * outputs,
        scratch_shapes=[
            pltpu.VMEM((rows, width), jnp.float32),
            pltpu.SemaphoreType.DMA((blocks,)),
        ],
        compiler_params=room(4),
        name="pairs",
    )(place, pltpu.with_memory_space_constraint(matrix, pltpu.HBM))


def three_pass(high, low, right_high, right_low):
    dot = functools.partial(jnp.dot, preferred_element_type=jnp.float32)
    rows = high.shape[0]
    both = dot(jnp.concatenate([high, low]), right_high)
    return both[:rows] + both[rows:] + dot(high, right_low)


def adjoint_kernel(
    kept_ref, given_ref, kept_high_ref, kept_low_ref, given_high_ref, given_low_ref, *out_refs,
    first, block,
):
    width = given_ref.shape[1]
    slot = width // 2
    for out_ref in out_refs:
        out_ref[...] = jnp.zeros(out_ref.shape, jnp.float32)

    def body(i, carry):
        here = pl.ds(pl.multiple_of(i * block, block), block)
        kept = split(kept_ref[here, first : first + width].T)
        given = split(given_ref[here, :].T)
        total = three_pass(
            *kept, kept_high_ref[here, :], kept_low_ref[here, :]
        ) + three_pass(*given, given_high_ref[here, :], given_low_ref[here, :])
        for i, out_ref in enumerate(out_refs):
            out_ref[...] += total[i * slot : (i + 1) * slot]
        return carry

    lax.fori_loop(0, given_ref.shape[0] // block, body, 0)


def adjoint_of(kept, first, given, own_window, other_window):
    operands = [resident(kept), given, *(resident(value) for value in (*own_window, *other_window))]
    return pl.pallas_call(
        functools.partial(adjoint_kernel, first=first, block=256),
        out_shape=[pltpu.VMEM((given.shape[1] // 2, own_window[0].shape[1]), jnp.float32)] * 2,
        in_specs=[VMEM] * len(operands),
        out_specs=[VMEM] * 2,
        compiler_params=room(8),
        name="adjoint",
    )(*operands)


def early_kernel(*refs, parts):
    out_ref, high_ref, low_ref = refs[-3:]
    fill(high_ref, low_ref, refs[:parts])
    block = 256

    def body(i, carry):
        here = pl.ds(pl.multiple_of(i * block, block), block)
        high, low = split(jnp.concatenate([ref[here, :] for ref in refs[parts:-3]], axis=1))
        out_ref[here, :] = three_pass(high, low, high_ref[...], low_ref[...])
        return carry

    lax.fori_loop(0, out_ref.shape[0] // block, body, 0)


def early_of(kernels, parts):
    width = sum(kernel.shape[1] for kernel in kernels)
    columns = parts[0].shape[1]
    operands = [resident(value) for value in (*parts, *kernels)]
    return pl.pallas_call(
        functools.partial(early_kernel, parts=len(parts)),
        out_shape=pltpu.VMEM((kernels[0].shape[0], columns), jnp.float32),
        in_specs=[VMEM] * len(operands),
        out_specs=VMEM,
        scratch_shapes=[pltpu.VMEM((width, columns), jnp.bfloat16)] * 2,
        compiler_params=room(8),
        name="early",
    )(*operands)


def fill(high_ref, low_ref, parts):
    start = 0
    for part in parts:
        here = slice(start, start + part.shape[0])
        high_ref[here, :], low_ref[here, :] = split(part[...])
        start += part.shape[0]


def forward_kernel(*refs, parts, group, vectors, lags, steps):
    before_ref, out_ref, high_ref, low_ref, product_ref, rows_ref = refs[-6:]
    blocks = before_ref.shape[0] // (group * lags)
    fill(high_ref, low_ref, refs[:parts])

    def multiply(block):
        here = pl.ds(pl.multiple_of(block * group * lags, group * lags), group * lags)
        high, low = split(jnp.concatenate([ref[here, :] for ref in refs[parts:-6]], axis=1))
        product_ref[lax.rem(block, 2)] = before_ref[here, :] + three_pass(
            high, low, high_ref[...], low_ref[...]
        )

    def shear(block):
        for s in range(group):
            for b in range(vectors):
                tile = product_ref[
                    lax.rem(block, 2), s * lags : (s + 1) * lags, b * steps : (b + 1) * steps
                ]
                rows_ref[pl.ds((block * group + s) * vectors + b, 1), :] = jnp.sum(
                    skewed(tile), axis=0, keepdims=True
                )

    multiply(0)

    def body(block, carry):
        shear(block - 1)
        multiply(block)
        return carry

    lax.fori_loop(1, blocks, body, 0)
    shear(blocks - 1)
    out_ref[...] = rows_ref[...].T


def forward_of(kernels, parts, before, lags, vectors):
    rows, columns = before.shape
    width = sum(kernel.shape[1] for kernel in kernels)
    steps = columns // vectors
    sensors = rows // lags
    group = 8
    operands = [resident(value) for value in (*parts, *kernels, before)]
    return pl.pallas_call(
        functools.partial(
            forward_kernel, parts=len(parts), group=group, vectors=vectors, lags=lags, steps=steps
        ),
        out_shape=pltpu.VMEM((steps, sensors * vectors), jnp.float32),
        in_specs=[VMEM] * len(operands),
        out_specs=VMEM,
        scratch_shapes=[
            pltpu.VMEM((width, columns), jnp.bfloat16),
            pltpu.VMEM((width, columns), jnp.bfloat16),
            pltpu.VMEM((2, group * lags, columns), jnp.float32),
            pltpu.VMEM((sensors * vectors, steps), jnp.float32),
        ],
        compiler_params=room(12),
        name="forward",
    )(*operands)


def smooth_kernel(place_ref, series_ref, taps_ref, out_ref, *, vectors, steps):
    taps = taps_ref.shape[0]
    rows = series_ref.shape[0]
    half = (taps - 1) // 2
    slot = place_ref[0] * (taps_ref.shape[1] // (2 * rows)) + place_ref[1]
    pair = taps_ref[:, pl.ds(pl.multiple_of(slot // 2 * 2 * rows, 2 * rows), 2 * rows)]
    weights = pltpu.roll(pair, lax.rem(slot, 2) * rows, 1).T[:rows]
    turn = mirror(steps)
    lane = lax.broadcasted_iota(jnp.int32, (rows, steps), 1)
    for b in range(vectors):
        block = jnp.dot(
            series_ref[:, b * steps : (b + 1) * steps], turn, precision=lax.Precision.HIGHEST
        )
        total = weights[:, half : half + 1] * block
        for k in range(taps):
            move = k - half
            if move == 0:
                continue
            moved = pltpu.roll(block, (-move) % steps, 1)
            inside = lane < steps - move if move > 0 else lane >= -move
            total = total + weights[:, k : k + 1] * jnp.where(inside, moved, 0.0)
        out_ref[:, b * steps : (b + 1) * steps] = total


def smooth_of(series, taps, place, vectors):
    columns = series.shape[1]
    return pl.pallas_call(
        functools.partial(smooth_kernel, vectors=vectors, steps=columns // vectors),
        out_shape=pltpu.VMEM(series.shape, jnp.float32),
        in_specs=[pl.BlockSpec(memory_space=pltpu.SMEM), VMEM, VMEM],
        out_specs=VMEM,
        compiler_params=room(4),
        name="smooth",
    )(place, resident(series), resident(taps))


def send_z(value, step):
    return lax.ppermute(value, "z", ring(lax.axis_size("z"), step))


def reduce_over_z(addend_of):
    far = lax.axis_size("z") // 2
    value = addend_of(far)
    cut = value.shape[0] // 2
    up = send_z(value[:cut], 1)
    down = send_z(value[cut:], -1)
    above, below = addend_of(far - 1), addend_of(1 - far)
    up = jnp.concatenate([above[:cut] + up, above[cut:]])
    down = jnp.concatenate([below[:cut], below[cut:] + down])
    for offset in range(far - 2, -1, -1):
        up = send_z(up, 1)
        down = send_z(down, -1)
        if offset:
            up = up + addend_of(offset)
            down = down + addend_of(-offset)
    return addend_of(0) + up + down


def gather_over_z(own):
    far = lax.axis_size("z") // 2
    cut = own.shape[0] // 2
    up, down = own, own
    parts = {0: own}
    for step in range(1, far):
        up = send_z(up, 1)
        down = send_z(down, -1)
        parts[-step], parts[step] = up, down
    up = send_z(up[:cut], 1)
    down = send_z(down[cut:], -1)
    parts[far] = jnp.concatenate([up, down])
    return parts


def gather_over_y(series, low):
    other = swap(series, "yl")
    both = jnp.stack([series, other])
    other = lax.ppermute(both, ("yl", "yh"), [(i, 3 - i) for i in range(4)])[::-1]
    return jnp.stack([jnp.where(low, both, other), jnp.where(low, other, both)])


def gather_over_x(pieces, first, even, low):
    other = swap(pieces, "c")
    here = jnp.stack([jnp.where(first, pieces, other), jnp.where(first, other, pieces)], 2)
    here = jnp.swapaxes(here, 0, 1)
    size = lax.axis_size("x")
    other = lax.ppermute(here, "x", [(i, i ^ 1) for i in range(size)])
    pair = jnp.stack([jnp.where(even, here, other), jnp.where(even, other, here)], 1)
    other = lax.ppermute(pair, "x", [(i, size - 1 - i) for i in range(size)])
    whole = jnp.stack([jnp.where(low, pair, other), jnp.where(low, other, pair)], 1)
    return whole.reshape(whole.shape[0], -1, whole.shape[-1])


def reduce_over_unk(result):
    size = lax.axis_size(UNK)
    pieces = result.reshape(size, result.shape[0] // size, result.shape[1])
    return jnp.sum(lax.all_to_all(pieces, UNK, 0, 0, tiled=True), axis=0)


def action(signals, kernel, tap_weights):
    sensors, vectors, steps_here = signals.shape
    lags, unknowns = kernel.shape[1:]
    z_size = lax.axis_size("z")
    x, yh, c = (lax.axis_index(name) for name in UNK)
    place = jnp.stack([lax.axis_index("yl"), lax.axis_index("z")]).astype(jnp.int32)
    signals, place, lower, *sides = lax.optimization_barrier(
        (signals, place, yh == 0, c == 0, lax.rem(x, 2) == 0, x < 2)
    )
    slot = unknowns // (2 * z_size)
    matrix = kernel.reshape(sensors * lags, unknowns)

    pieces = gather_over_y(signals.reshape(sensors * vectors, steps_here).T, lower)
    given, kept = [], []
    for i in range(2):
        pairs = PAIRS[2 * i : 2 * i + 2]
        sent = pairs_of(matrix, place, True, pairs, 2)
        for block in sent:
            given.append(swap(block, "yl"))
        kept += pairs_of(matrix, place, False, pairs, 1)
    series = gather_over_x(pieces, *sides)
    own_window = window_of(series[0], lags, vectors)
    other_window = window_of(series[1], lags, vectors)
    addends = {}
    for i, pair in enumerate(PAIRS):
        addends[pair[0]], addends[pair[1]] = adjoint_of(
            kept[i // 2], i % 2 * 2 * slot, given[i], own_window, other_window
        )
    addends = smooth_of(
        reduce_over_z(lambda k: addends[k % z_size]), tap_weights, place, vectors
    )
    smoothed = gather_over_z(addends)

    def parts_of(pairs):
        return [smoothed[k if k <= z_size // 2 else k - z_size] for pair in pairs for k in pair]

    parts = parts_of(PAIRS[2:])
    other = early_of(given[2:], parts)
    own = early_of(kept[1:], parts)
    parts = parts_of(PAIRS[:2])
    other = forward_of(given[:2], parts, other, lags, vectors)
    own = forward_of(kept[:1], parts, own, lags, vectors)
    result = reduce_over_unk(own + swap(other, "yl"))
    return result.T.reshape(sensors, vectors, steps_here)


def solution(mesh):
    sens, unk = mesh.devices.shape
    fine = Mesh(mesh.devices.reshape(sens // 2, 2, unk // 4, 2, 2), ("z", "yl", *UNK))
    sensor_axes = ("z", "yl")
    return jax.shard_map(
        action,
        mesh=fine,
        in_specs=(P(sensor_axes, None, UNK), P(sensor_axes, None, UNK), P(None, UNK)),
        out_specs=P(sensor_axes, None, UNK),
        check_vma=False,
    )
```
